32 devices in a mesh: gx: 4 (over x, core), gy: 2 (over y), gz: 4 (over z).
Axes of the slice: x: 2, y: 2, z: 4, core: 2. Of those that a mesh axis runs over, the one named last changes fastest.
Arguments:
- coarse_pdfs: float32 [19, 16, 8, 256], P(None, 'gx', 'gy', 'gz'), may hold values from 0.1 to 32
- fine_pdfs: float32 [19, 16, 16, 512], P(None, 'gx', 'gy', 'gz'), may hold values from 0.1 to 32
- centers: int32 [3, 3, 1, 1, 8], replicated, may hold values from 4 to 59, as said below
- sphere_velocity: float32 [3, 1, 1, 8], replicated, may hold values from -0.05 to 0.05
Outputs:
- coarse_next: float32 [19, 16, 8, 256], P(None, 'gx', 'gy', 'gz')
- fine_next: float32 [19, 16, 16, 512], P(None, 'gx', 'gy', 'gz')
- sphere_force: float32 [2, 3, 1, 1, 8], replicated
The draws below stay inside these ranges and needn't reach their ends.
Inputs may be any that keep to these rules, and one draw needn't show every extreme that they name: `centers`: each coordinate of a center is counted from its box's first cell; from one substep to the next it changes by -1, 0 or 1, and the same change repeats in the second substep.
All inputs are finite; a program needn't handle non-finite values.
Results may differ from the reference program's by a relative error of at most 0.0003.
Values sent between devices are 32-bit elements; how exact they have to be, the bound alone decides.
A program may use at most 64 MiB of HBM per device.

```python
import jax
import jax.numpy as jnp
from jax import lax

BOX_XY = 16
BOX_Z = 64
RADIUS = 4
NX = 16
NY = 8
NZ = 256
FINE_X = 16
FINE_Y = 16
FINE_Z = 512
NBX = 1
NBY = 1
NBZ = 8


VELOCITIES = ((0, 0, 0), (1, 0, 0), (-1, 0, 0), (0, 1, 0), (0, -1, 0), (0, 0, 1), (0, 0, -1), (1, 1, 0), (-1, -1, 0), (1, -1, 0), (-1, 1, 0), (1, 0, 1), (-1, 0, -1), (1, 0, -1), (-1, 0, 1), (0, 1, 1), (0, -1, -1), (0, 1, -1), (0, -1, 1))


WEIGHTS = (1.0 / 3.0,) + (1.0 / 18.0,) * 6 + (1.0 / 36.0,) * 12


def population_field(key, extent_x, extent_y, extent_z):
    subkeys = jax.random.split(key, 3)
    density = jax.random.uniform(subkeys[0], (extent_x, extent_y, extent_z), jnp.float32, 20.0, 52.0)
    velocity = jax.random.uniform(subkeys[1], (3, extent_x, extent_y, extent_z), jnp.float32, -0.06, 0.06)
    jitter = jax.random.uniform(subkeys[2], (19, extent_x, extent_y, extent_z), jnp.float32, -0.3, 0.3)
    speed_sq = velocity[0] * velocity[0] + velocity[1] * velocity[1] + velocity[2] * velocity[2]
    populations = []
    for direction in range(19):
        projected = VELOCITIES[direction][0] * velocity[0] + VELOCITIES[direction][1] * velocity[1] + VELOCITIES[direction][2] * velocity[2]
        populations.append(WEIGHTS[direction] * density * (1.0 + 3.0 * projected + 4.5 * projected * projected - 1.5 * speed_sq + jitter[direction]))
    return jnp.stack(populations)


def draw_coarse_pdfs(key, part):
    return population_field(jax.random.fold_in(key, 101), NX, NY, NZ)


def draw_fine_pdfs(key, part):
    return population_field(jax.random.fold_in(key, 202), FINE_X, FINE_Y, FINE_Z)


def draw_centers(key, part):
    subkeys = jax.random.split(jax.random.fold_in(key, 303), 2)
    limits = jnp.array([BOX_XY, BOX_XY, BOX_Z], dtype=jnp.int32)[:, None, None, None]
    starts = jax.random.randint(subkeys[0], (3, NBX, NBY, NBZ), RADIUS + 2, limits - RADIUS - 2, dtype=jnp.int32)
    motion = jax.random.randint(subkeys[1], (3, NBX, NBY, NBZ), -1, 2, dtype=jnp.int32)
    return jnp.stack([starts, starts + motion, starts + 2 * motion])


def setup_inputs(seed: int = 0) -> dict:
    splits = jax.random.split(jax.random.key(seed), 5)
    coarse_pdfs = draw_coarse_pdfs(jax.random.fold_in(splits[4], 71), 0)
    fine_pdfs = draw_fine_pdfs(jax.random.fold_in(splits[4], 71), 0)
    centers = draw_centers(jax.random.fold_in(splits[4], 71), 0)
    sphere_velocity = jnp.clip(jax.random.uniform(splits[3], (3, NBX, NBY, NBZ), jnp.float32, -0.05, 0.05), -0.05, 0.05)
    return {"coarse_pdfs": coarse_pdfs, "fine_pdfs": fine_pdfs, "centers": centers, "sphere_velocity": sphere_velocity}


VELOCITIES = ((0, 0, 0), (1, 0, 0), (-1, 0, 0), (0, 1, 0), (0, -1, 0), (0, 0, 1), (0, 0, -1), (1, 1, 0), (-1, -1, 0), (1, -1, 0), (-1, 1, 0), (1, 0, 1), (-1, 0, -1), (1, 0, -1), (-1, 0, 1), (0, 1, 1), (0, -1, -1), (0, 1, -1), (0, -1, 1))
OPPOSITE = (0, 2, 1, 4, 3, 6, 5, 8, 7, 10, 9, 12, 11, 14, 13, 16, 15, 18, 17)
WEIGHTS = (1.0 / 3.0,) + (1.0 / 18.0,) * 6 + (1.0 / 36.0,) * 12
COARSE_RATE = 1.25
FINE_RATE = 1.0 / 1.1
HIGHEST = lax.Precision.HIGHEST


def project(vectors, direction):
    projected = jnp.zeros_like(vectors[0])
    for dimension in range(3):
        sign = VELOCITIES[direction][dimension]
        if sign == 1:
            projected = projected + vectors[dimension]
        elif sign == -1:
            projected = projected - vectors[dimension]
    return projected


def speed_squared(vectors):
    return vectors[0] * vectors[0] + vectors[1] * vectors[1] + vectors[2] * vectors[2]


def equilibrium(density, vectors, speed_sq, direction):
    projected = project(vectors, direction)
    return WEIGHTS[direction] * density * (1.0 + 3.0 * projected + 4.5 * projected * projected - 1.5 * speed_sq)


def total_density(populations):
    density = populations[0]
    for direction in range(1, 19):
        density = density + populations[direction]
    return density


def collide(populations, relaxation):
    density = total_density(populations)
    velocity = []
    for dimension in range(3):
        summed = jnp.zeros_like(density)
        for direction in range(19):
            sign = VELOCITIES[direction][dimension]
            if sign == 1:
                summed = summed + populations[direction]
            elif sign == -1:
                summed = summed - populations[direction]
        velocity.append(summed / density)
    speed_sq = speed_squared(velocity)
    relaxed = []
    for direction in range(19):
        target = equilibrium(density, velocity, speed_sq, direction)
        relaxed.append(populations[direction] - relaxation * (populations[direction] - target))
    return jnp.stack(relaxed)


def box_onehot(coords, box_size, box_count):
    box_index = jnp.floor_divide(coords, box_size)
    onehot = (box_index[None, :] == jnp.arange(box_count, dtype=jnp.int32)[:, None]).astype(jnp.float32)
    offsets = (coords - box_index * box_size).astype(jnp.float32)
    return onehot, offsets


def geometry(coord_x, coord_y, coord_z, centers, sphere_velocity):
    count_x, count_y, count_z = centers.shape[2], centers.shape[3], centers.shape[4]
    table_x, offset_x = box_onehot(coord_x, BOX_XY, count_x)
    table_y, offset_y = box_onehot(coord_y, BOX_XY, count_y)
    table_z, offset_z = box_onehot(coord_z, BOX_Z, count_z)
    inside = ((coord_x >= 0) & (coord_x < count_x * BOX_XY))[:, None, None]

    def spread(values):
        return jnp.einsum("abc,ax,by,cz->xyz", values, table_x, table_y, table_z, precision=HIGHEST)

    solids = []
    for moment in range(3):
        gap_x = offset_x[:, None, None] - spread(centers[moment, 0].astype(jnp.float32))
        gap_y = offset_y[None, :, None] - spread(centers[moment, 1].astype(jnp.float32))
        gap_z = offset_z[None, None, :] - spread(centers[moment, 2].astype(jnp.float32))
        distance = gap_x * gap_x + gap_y * gap_y + gap_z * gap_z
        solids.append((distance <= float(RADIUS * RADIUS)) & inside)
    velocity_field = [spread(sphere_velocity[dimension]) for dimension in range(3)]
    return solids, velocity_field


def pull_from(values, direction):
    step_x, step_y, step_z = VELOCITIES[direction]
    width_x = values.shape[-3] - 2
    sliced = values[..., 1 - step_x:1 - step_x + width_x, :, :]
    return jnp.roll(sliced, (step_y, step_z), axis=(-2, -1))


def upsample(ghost_plane):
    return jnp.repeat(jnp.repeat(ghost_plane, 2, axis=1), 2, axis=2)


def coalesce(ghost_plane):
    grouped = ghost_plane.reshape(19, ghost_plane.shape[1] // 2, 2, ghost_plane.shape[2] // 2, 2)
    return (grouped[:, :, 0, :, 0] + grouped[:, :, 1, :, 0] + grouped[:, :, 0, :, 1] + grouped[:, :, 1, :, 1]) * 0.25


def substep(padded, solid_prev, solid_new, velocity_field):
    interior = padded[:, 1:-1]
    density = total_density(padded)
    density_in = density[1:-1]
    open_cells = jnp.logical_not(solid_prev) & jnp.logical_not(solid_new)
    moving = open_cells[1:-1]
    numerator = WEIGHTS[0] * density_in
    denominator = jnp.full(density_in.shape, WEIGHTS[0], jnp.float32)
    arrived = [interior[0]]
    push_sums = [jnp.zeros(density_in.shape, jnp.float32) for dimension in range(3)]
    for direction in range(1, 19):
        step_x, step_y, step_z = VELOCITIES[direction]
        solid_next = pull_from(solid_new, direction)
        neighbour_velocity = [pull_from(values, direction) for values in velocity_field]
        returned = interior[OPPOSITE[direction]]
        bounced = returned + 6.0 * WEIGHTS[direction] * density_in * project(neighbour_velocity, direction)
        arrived.append(jnp.where(solid_next, bounced, pull_from(padded[direction], direction)))
        link_term = jnp.where(solid_next & moving, returned + bounced, 0.0)
        pushed = jnp.roll(link_term, (-step_x, -step_y, -step_z), axis=(0, 1, 2))
        for dimension in range(3):
            sign = VELOCITIES[direction][dimension]
            if sign == 1:
                push_sums[dimension] = push_sums[dimension] - pushed
            elif sign == -1:
                push_sums[dimension] = push_sums[dimension] + pushed
        open_next = pull_from(open_cells, direction).astype(jnp.float32)
        numerator = numerator + WEIGHTS[direction] * pull_from(density, direction) * open_next
        denominator = denominator + WEIGHTS[direction] * open_next
    refill_density = numerator / denominator
    own_velocity = [values[1:-1] for values in velocity_field]
    speed_sq = speed_squared(own_velocity)
    covered = solid_new[1:-1]
    uncovered = solid_prev[1:-1]
    updated = []
    for direction in range(19):
        refill = equilibrium(refill_density, own_velocity, speed_sq, direction)
        updated.append(jnp.where(covered, interior[direction], jnp.where(uncovered, refill, arrived[direction])))
    stacked = jnp.stack(push_sums).reshape(3, NBX, BOX_XY, NBY, BOX_XY, NBZ, BOX_Z)
    forces = jnp.sum(stacked, axis=(2, 4, 6))
    return jnp.stack(updated), forces


def reference(coarse_pdfs, fine_pdfs, centers, sphere_velocity):
    coord_x = jnp.arange(-1, FINE_X + 1, dtype=jnp.int32)
    coord_y = jnp.arange(FINE_Y, dtype=jnp.int32)
    coord_z = jnp.arange(FINE_Z, dtype=jnp.int32)
    solids, velocity_field = geometry(coord_x, coord_y, coord_z, centers, sphere_velocity)
    coarse_post = collide(coarse_pdfs, COARSE_RATE)
    left_fill = upsample(coarse_post[:, NX - 1])
    right_fill = upsample(coarse_post[:, 0])
    first_post = collide(fine_pdfs, FINE_RATE)
    left_coal = coalesce(first_post[:, FINE_X - 1])
    right_coal = coalesce(first_post[:, 0])

    def extended(fresh):
        return jnp.concatenate([left_fill[:, None], fresh, right_fill[:, None]], axis=1)

    middle, first_forces = substep(extended(first_post), solids[0], solids[1], velocity_field)
    fine_next, second_forces = substep(extended(collide(middle, FINE_RATE)), solids[1], solids[2], velocity_field)
    coarse_ready = jnp.concatenate([left_coal[:, None], coarse_post, right_coal[:, None]], axis=1)
    coarse_next = jnp.stack([pull_from(coarse_ready[direction], direction) for direction in range(19)])
    return coarse_next, fine_next, jnp.stack([first_forces, second_forces])
```

```python
import functools

import jax
import jax.numpy as jnp
from jax import lax
from jax.experimental import pallas as pl
from jax.experimental.pallas import tpu as pltpu
from jax.sharding import PartitionSpec as P

BOX_XY = 16
BOX_Z = 64
RADIUS = 4
VELOCITIES = (
    (0, 0, 0),
    (1, 0, 0),
    (-1, 0, 0),
    (0, 1, 0),
    (0, -1, 0),
    (0, 0, 1),
    (0, 0, -1),
    (1, 1, 0),
    (-1, -1, 0),
    (1, -1, 0),
    (-1, 1, 0),
    (1, 0, 1),
    (-1, 0, -1),
    (1, 0, -1),
    (-1, 0, 1),
    (0, 1, 1),
    (0, -1, -1),
    (0, 1, -1),
    (0, -1, 1),
)
OPPOSITE = (0, 2, 1, 4, 3, 6, 5, 8, 7, 10, 9, 12, 11, 14, 13, 16, 15, 18, 17)
WEIGHTS = (1.0 / 3.0,) + (1.0 / 18.0,) * 6 + (1.0 / 36.0,) * 12
COARSE_RATE = 1.25
FINE_RATE = 1.0 / 1.1
HIGHEST = lax.Precision.HIGHEST
MESH = pl.DeviceIdType.MESH
AXES = ("gx", "gy", "gz")
DIRS = VELOCITIES[1:]
RHO = 5
MOVERS = {
    (axis, sign): tuple(q for q in range(19) if VELOCITIES[q][axis] == sign)
    for axis in range(3)
    for sign in (1, -1)
}
SLOT = {1: 0, -1: 1}
PAIRS = ((1, 1), (1, -1), (-1, 1), (-1, -1))
PAIR_SLOT = {pair: i for i, pair in enumerate(PAIRS)}
FIRST_ROW = 8
COARSE_ROW = 32
ROWS = 52
LANES = 128
SUB = 8


def iota(shape, axis):
    return lax.broadcasted_iota(jnp.int32, shape, axis)


def project(vectors, direction):
    total = None
    for dim in range(3):
        sign = VELOCITIES[direction][dim]
        if sign == 1:
            total = vectors[dim] if total is None else total + vectors[dim]
        elif sign == -1:
            total = -vectors[dim] if total is None else total - vectors[dim]
    return total


def collide(read, write, rate):
    density = read(0)
    momentum = [None, None, None]
    for q in range(1, 19):
        value = read(q)
        density = density + value
        for dim in range(3):
            sign = VELOCITIES[q][dim]
            if sign:
                if momentum[dim] is None:
                    momentum[dim] = value if sign == 1 else -value
                else:
                    momentum[dim] = momentum[dim] + value if sign == 1 else momentum[dim] - value
    inverse = 1.0 / density
    velocity = [m * inverse for m in momentum]
    base = 1.0 - 1.5 * (
        velocity[0] * velocity[0] + velocity[1] * velocity[1] + velocity[2] * velocity[2]
    )
    scaled = {w: (rate * w) * density for w in set(WEIGHTS)}
    keep = 1.0 - rate
    write(0, keep * read(0) + scaled[WEIGHTS[0]] * base)
    for q in range(1, 19, 2):
        along = project(velocity, q)
        even = base + 4.5 * along * along
        odd = 3.0 * along
        weight = scaled[WEIGHTS[q]]
        write(q, keep * read(q) + weight * (even + odd))
        write(q + 1, keep * read(q + 1) + weight * (even - odd))
    return density


class Halo:
    def __init__(self, send, recv):
        self.sx, self.sy, self.sz = send
        self.rx, self.ry, self.rz, self.rxy, self.rxz, self.ryz = recv

    def pack(self, own, edge_planes, with_rho, rows, lanes, part):
        x0 = 0 if part == 0 else 6
        y0 = FIRST_ROW if part == 0 else COARSE_ROW
        lane = iota((SUB, LANES), 1)
        for sign in (1, -1):
            for k, q in enumerate(MOVERS[0, sign] + ((RHO + 100,) if with_rho else ())):
                self.sx[SLOT[sign], x0 + k] = edge_planes[sign](q)
        for sign in (1, -1):
            row = rows - 1 if sign == 1 else 0
            out = SLOT[sign]
            for k, q in enumerate(MOVERS[1, sign] + ((RHO + 100,) if with_rho else ())):
                self.sy[out, y0 + 4 * k : y0 + 4 * k + 4] = own(q)[:, row : row + 1, :]
            for e, xs in enumerate((1, -1)):
                q = VELOCITIES.index((xs, sign, 0))
                if part == 0:
                    self.sy[out, 2 * e] = edge_planes[xs](q)[row : row + 1, :]
                    self.sy[out, 2 * e + 1] = edge_planes[xs](RHO + 100)[row : row + 1, :]
                else:
                    self.sy[out, 4 + e] = edge_planes[xs](q)[row : row + 1, :]
        for sign in (1, -1):
            source = lanes - 1 if sign == 1 else 0
            packed = jnp.zeros((SUB, LANES), jnp.float32)
            for k, q in enumerate(MOVERS[2, sign] + ((RHO + 100,) if with_rho else ())):
                value = own(q)
                for j in range(4):
                    place = k * 6 + j + 1
                    moved = pltpu.roll(value[j], (place - source) % LANES, 1)
                    packed = jnp.where(lane == place, moved, packed)
                for xs, place in ((1, k * 6 + 5), (-1, k * 6)):
                    if q == RHO + 100 or VELOCITIES[q][0] == xs:
                        moved = pltpu.roll(edge_planes[xs](q), (place - source) % LANES, 1)
                        packed = jnp.where(lane == place, moved, packed)
            self.sz[SLOT[sign], part] = packed

    def pull(self, own, c, q, rows, lanes, part):
        cx, cy, cz = c
        is_rho = q == RHO + 100
        x0 = 0 if part == 0 else 6
        y0 = FIRST_ROW if part == 0 else COARSE_ROW

        def index(axis, sign):
            return RHO if is_rho else MOVERS[axis, sign].index(q)

        def along_x(inner, halo):
            if cx == 1:
                return jnp.concatenate([halo, inner[:3]], axis=0)
            return jnp.concatenate([inner[1:], halo], axis=0)

        value = own
        row = iota((1, SUB, 1), 1)
        if cx:
            value = along_x(own, self.rx[SLOT[cx], x0 + index(0, cx)][None])
        if cy:
            edge = 0 if cy == 1 else rows - 1
            k = y0 + 4 * index(1, cy)
            lines = self.ry[SLOT[cy], k : k + 4]
            if cx:
                e = 0 if cx == 1 else 1
                at = (2 * e + (1 if is_rho else 0)) if part == 0 else 4 + e
                lines = along_x(lines, self.rxy[PAIR_SLOT[cx, cy], at : at + 1])
            value = jnp.where(row == edge, lines, pltpu.roll(value, cy % SUB, 1))
        if cz:
            edge = 0 if cz == 1 else lanes - 1
            k = index(2, cz) * 6
            packed = self.rz[SLOT[cz], part]
            if cy:
                source_row = rows - 1 if cy == 1 else 0
                other = self.ryz[PAIR_SLOT[cy, cz], part][source_row : source_row + 1, :]
                edge_row = 0 if cy == 1 else rows - 1
                packed = jnp.where(
                    iota((SUB, 1), 0) == edge_row, other, pltpu.roll(packed, cy % SUB, 0)
                )
            columns = []
            for ix in range(4):
                j = ix - cx
                if 0 <= j < 4:
                    columns.append(pltpu.roll(packed, (edge - (k + j + 1)) % LANES, 1))
                else:
                    other = self.rxz[PAIR_SLOT[cx, cz], part]
                    place = k + 5 if cx == 1 else k
                    columns.append(pltpu.roll(other, (edge - place) % LANES, 1))
            columns = jnp.stack(columns)
            lane = iota((1, 1, LANES), 2)
            value = jnp.where(lane == edge, columns, pltpu.roll(value, cz % LANES, 2))
        return value


def neighbour(c, counts, me):
    return tuple(lax.rem(me[a] + c[a] + counts[a], counts[a]) for a in range(3))


def kernel(
    counts,
    coarse_in,
    fine_in,
    centers,
    speeds,
    coarse_out,
    fine_out,
    force_out,
    fine_a,
    fine_b,
    coarse,
    sx1,
    sy1,
    sz1,
    rx1,
    ry1,
    rz1,
    rxy1,
    rxz1,
    ryz1,
    sx2,
    sy2,
    sz2,
    rx2,
    ry2,
    rz2,
    rxy2,
    rxz2,
    ryz2,
    opens,
    news,
    own_masks,
    dens,
    fill_ref,
    force_own,
    force_x,
    force_y,
    force_z,
    send_sem,
    recv_sem,
    fsend_sem,
    frecv_x,
    frecv_y,
    frecv_z,
):
    me = tuple(lax.axis_index(a) for a in AXES)
    own_x, own_y, own_z = fine_in.shape[1], fine_in.shape[2], fine_in.shape[3]
    rows_c, lanes_c = coarse_in.shape[2], coarse_in.shape[3]
    total_x = own_x * counts[0]
    box_x, box_y, box_z = centers.shape[2], centers.shape[3], centers.shape[4]
    local_z = own_z // BOX_Z

    barrier = pltpu.get_barrier_semaphore()
    for c in DIRS:
        pl.semaphore_signal(
            barrier, inc=1, device_id=neighbour(c, counts, me), device_id_type=MESH
        )
    for axis in range(3):
        for step in range(1, counts[axis]):
            c = tuple(step if a == axis else 0 for a in range(3))
            pl.semaphore_signal(
                barrier, inc=1, device_id=neighbour(c, counts, me), device_id_type=MESH
            )

    def write_a(q, value):
        fine_a[q] = value

    rho = collide(lambda q: fine_in[q], write_a, FINE_RATE)
    coarse[...] = jnp.ones(coarse.shape, jnp.float32)
    coarse[:, :, 0:rows_c, 0:lanes_c] = coarse_in[...]

    def write_c(q, value):
        coarse[q] = value

    rho_c = collide(lambda q: coarse[q], write_c, COARSE_RATE)
    first = me[0] == 0
    last = me[0] == counts[0] - 1
    row3 = iota((1, SUB, 1), 1)

    planes = []
    for sign, ix in ((1, 3), (-1, 0)):
        planes += [coarse[q, ix] for q in MOVERS[0, sign]] + [rho_c[ix]]
    grow = (iota((LANES, LANES), 0) == (iota((LANES, LANES), 1) >> 1)).astype(jnp.float32)
    wide = jnp.dot(
        jnp.concatenate(planes, axis=0), grow, precision=HIGHEST, preferred_element_type=jnp.float32
    ).reshape(12, SUB, LANES)
    tall = wide[:, 3:4, :]
    for r in (2, 1, 0):
        tall = jnp.where(row3 < 2 * r + 2, wide[:, r : r + 1, :], tall)
    fill_ref[...] = tall

    planes = []
    for sign, ix in ((1, 3), (-1, 0)):
        for q in MOVERS[0, sign]:
            plane = fine_a[q, ix]
            planes.append(plane + pltpu.roll(plane, SUB - 1, 0))
    shrink = 0.25 * ((iota((LANES, LANES), 0) >> 1) == iota((LANES, LANES), 1)).astype(jnp.float32)
    thin = jnp.dot(
        jnp.concatenate(planes, axis=0),
        shrink,
        precision=HIGHEST,
        preferred_element_type=jnp.float32,
    ).reshape(10, SUB, LANES)
    flat = thin[:, 6:7, :]
    for r in (2, 1, 0):
        flat = jnp.where(row3 <= r, thin[:, 2 * r : 2 * r + 1, :], flat)

    def fine_edges(ref, density):
        def plane(sign):
            ix, at_end, base = (3, last, 0) if sign == 1 else (0, first, 6)

            def get(q):
                is_rho = q == RHO + 100
                k = RHO if is_rho else MOVERS[0, sign].index(q)
                mine = density[ix] if is_rho else ref[q, ix]
                return jnp.where(at_end, fill_ref[base + k], mine)

            return get

        return {1: plane(1), -1: plane(-1)}

    def coarse_edge(sign):
        ix, at_end, base = (3, last, 0) if sign == 1 else (0, first, 5)

        def get(q):
            return jnp.where(at_end, flat[base + MOVERS[0, sign].index(q)], coarse[q, ix])

        return get

    halo1 = Halo((sx1, sy1, sz1), (rx1, ry1, rz1, rxy1, rxz1, ryz1))
    halo2 = Halo((sx2, sy2, sz2), (rx2, ry2, rz2, rxy2, rxz2, ryz2))
    halo1.pack(
        lambda q: rho if q == RHO + 100 else fine_a[q],
        fine_edges(fine_a, rho),
        True,
        own_y,
        own_z,
        0,
    )
    halo1.pack(
        lambda q: coarse[q],
        {1: coarse_edge(1), -1: coarse_edge(-1)},
        False,
        rows_c,
        lanes_c,
        1,
    )

    def copies(halo, phase):
        made = []
        for i, c in enumerate(DIRS):
            cx, cy, cz = c
            if cz:
                if cx:
                    dst = halo.rxz.at[PAIR_SLOT[cx, cz]]
                elif cy:
                    dst = halo.ryz.at[PAIR_SLOT[cy, cz]]
                else:
                    dst = halo.rz.at[SLOT[cz]]
                src = halo.sz.at[SLOT[cz]]
            elif cy:
                if cx:
                    src = halo.sy.at[SLOT[cy], pl.ds(0, FIRST_ROW)]
                    dst = halo.rxy.at[PAIR_SLOT[cx, cy]]
                else:
                    src = halo.sy.at[SLOT[cy]]
                    dst = halo.ry.at[SLOT[cy]]
            else:
                src = halo.sx.at[SLOT[cx]]
                dst = halo.rx.at[SLOT[cx]]
            made.append(
                pltpu.make_async_remote_copy(
                    src_ref=src,
                    dst_ref=dst,
                    send_sem=send_sem.at[phase, i],
                    recv_sem=recv_sem.at[phase, i],
                    device_id=neighbour(c, counts, me),
                    device_id_type=MESH,
                )
            )
        return made

    pl.semaphore_wait(barrier, 18 + sum(n - 1 for n in counts))
    sends1 = copies(halo1, 0)
    for copy in sends1:
        copy.start()

    start_x, start_y, start_z = me[0] * own_x, me[1] * own_y, me[2] * own_z
    total_y = own_y * counts[1]
    bx0 = lax.div(start_x, BOX_XY)
    by0 = lax.div(start_y, BOX_XY)
    bz0 = me[2] * local_z
    bx_near = {
        1: lax.div(lax.max(start_x - 1, 0), BOX_XY),
        -1: lax.min(lax.div(start_x + own_x, BOX_XY), box_x - 1),
        0: bx0,
    }
    by_near = {
        1: lax.div(lax.rem(start_y + total_y - 1, total_y), BOX_XY),
        -1: lax.div(lax.rem(start_y + own_y, total_y), BOX_XY),
        0: by0,
    }
    bz_all = [lax.rem(bz0 + box_z + i, box_z) for i in range(-1, local_z + 1)]
    lane3 = iota((1, 1, LANES), 2)
    plane3 = iota((own_x, 1, LANES), 0)
    memo = {}

    def along_lanes(get, key, bx_key, by_key, cz):
        full = (key, bx_key, by_key, cz)
        if full in memo:
            return memo[full]
        bx, by = bx_near[bx_key], by_near[by_key]
        at = lane3 - cz
        value = jnp.full((1, 1, LANES), get(bx, by, bz_all[1]))
        for i in range(1, local_z):
            value = jnp.where(at >= i * BOX_Z, get(bx, by, bz_all[1 + i]), value)
        if cz == 1:
            value = jnp.where(at < 0, get(bx, by, bz_all[0]), value)
        elif cz == -1:
            value = jnp.where(at >= own_z, get(bx, by, bz_all[-1]), value)
        value = value.astype(jnp.float32)
        memo[full] = value
        return value

    def box_field(get, key, c):
        cx, cy, cz = c

        def on_rows(bx_key):
            own = along_lanes(get, key, bx_key, 0, cz)
            if cy == 0 or box_y == 1:
                return own
            edge = 0 if cy == 1 else own_y - 1
            return jnp.where(row3 == edge, along_lanes(get, key, bx_key, cy, cz), own)

        if cx == 0 or box_x == 1:
            return on_rows(0)
        edge = 0 if cx == 1 else own_x - 1
        return jnp.where(plane3 == edge, on_rows(cx), on_rows(0))

    def center_getter(moment, dim):
        return lambda bx, by, bz: centers[moment, dim, bx, by, bz]

    def speed_getter(dim):
        return lambda bx, by, bz: speeds[dim, bx, by, bz]

    def speeds_at(c):
        return [box_field(speed_getter(dim), ("u", dim), c) for dim in range(3)]

    def inside_at(cx):
        at = start_x + plane3 - cx
        return (at >= 0) & (at < total_x)

    def solids_at(c):
        cx, cy, cz = c
        off_x = ((start_x + plane3 - cx) & (BOX_XY - 1)).astype(jnp.float32)
        off_y = ((start_y + iota((1, SUB, LANES), 1) - cy) & (BOX_XY - 1)).astype(jnp.float32)
        off_z = ((lane3 - cz) & (BOX_Z - 1)).astype(jnp.float32)
        found = []
        for moment in range(3):
            gap_x = off_x - box_field(center_getter(moment, 0), (moment, 0), c)
            gap_y = off_y - box_field(center_getter(moment, 1), (moment, 1), c)
            gap_z = off_z - box_field(center_getter(moment, 2), (moment, 2), c)
            distance = (gap_x * gap_x + gap_z * gap_z) + gap_y * gap_y
            if cx:
                distance = jnp.where(inside_at(cx), distance, 1e9)
            found.append(jnp.where(distance <= float(RADIUS * RADIUS), 1.0, 0.0))
        return found

    own_solids = solids_at((0, 0, 0))
    for moment in range(3):
        own_masks[moment] = own_solids[moment]
    sums = [jnp.full((own_x, SUB, LANES), WEIGHTS[0], jnp.float32) for s in range(2)]
    for q in range(1, 19):
        s0, s1, s2 = solids_at(VELOCITIES[q])
        for s, (before, after) in enumerate(((s0, s1), (s1, s2))):
            free = (1.0 - before) * (1.0 - after)
            opens[s, q - 1] = free
            news[s, q - 1] = after
            sums[s] = sums[s] + WEIGHTS[q] * free
    for s in range(2):
        dens[s] = sums[s]
    own_speed = speeds_at((0, 0, 0))
    quiet = 1.0 - 1.5 * (
        own_speed[0] * own_speed[0] + own_speed[1] * own_speed[1] + own_speed[2] * own_speed[2]
    )

    def substep(s, halo, ref, density, write):
        covered = own_masks[s + 1] > 0.5
        uncovered = own_masks[s] > 0.5
        push = [jnp.zeros((own_x, SUB, LANES), jnp.float32) for d in range(3)]
        numerator = WEIGHTS[0] * density
        for q in range(1, 19):
            c = VELOCITIES[q]
            near = halo.pull(density, c, RHO + 100, own_y, own_z, 0)
            free = opens[s, q - 1]
            freed = near * free
            numerator = numerator + WEIGHTS[q] * freed
            arrived = halo.pull(ref[q], c, q, own_y, own_z, 0)
            here = (6.0 * WEIGHTS[q]) * project(own_speed, q)
            link = (2.0 * arrived - here * near) * free
            if c[0]:
                link = jnp.where(inside_at(c[0]), link, 0.0)
            for d in range(3):
                if c[d] == 1:
                    push[d] = push[d] + link
                elif c[d] == -1:
                    push[d] = push[d] - link
            wall = (6.0 * WEIGHTS[q]) * project(speeds_at(c), q)
            bounced = ref[OPPOSITE[q]] + density * wall
            arrived = jnp.where(news[s, q - 1] > 0.5, bounced, arrived)
            write(q, jnp.where(covered, ref[q], arrived))
        write(0, ref[0])
        refill = numerator / dens[s]
        replaced = uncovered & jnp.logical_not(covered)
        return refill, replaced, [jnp.where(covered, p, 0.0) for p in push]

    def refilled(refill, q):
        if q == 0:
            return refill * (WEIGHTS[0] * quiet)
        along = project(own_speed, q)
        return refill * (WEIGHTS[q] * (quiet + 3.0 * along + 4.5 * along * along))

    for copy in sends1:
        copy.wait_recv()

    def write_b(q, value):
        fine_b[q] = value

    refill, replaced, push1 = substep(0, halo1, fine_a, rho, write_b)
    for copy in sends1:
        copy.wait_send()

    def middle(q):
        return jnp.where(replaced, refilled(refill, q), fine_b[q])

    rho2 = collide(middle, write_a, FINE_RATE)
    halo2.pack(
        lambda q: rho2 if q == RHO + 100 else fine_a[q],
        fine_edges(fine_a, rho2),
        True,
        own_y,
        own_z,
        0,
    )
    sends2 = copies(halo2, 1)
    for copy in sends2:
        copy.start()

    for q in range(19):
        value = coarse[q]
        if q:
            value = halo1.pull(value, VELOCITIES[q], q, rows_c, lanes_c, 1)
        coarse_out[q] = value[:, 0:rows_c, 0:lanes_c]

    for copy in sends2:
        copy.wait_recv()

    def write_b2(q, value):
        fine_b[q] = value

    refill2, replaced2, push2 = substep(1, halo2, fine_a, rho2, write_b2)

    shape = force_own.shape[1:]
    row_at, lane_at = iota(shape, 0), iota(shape, 1)
    share = jnp.zeros(shape, jnp.float32)
    lane2 = iota((1, LANES), 1)
    for s, push in enumerate((push1, push2)):
        for d in range(3):
            column = jnp.sum(jnp.sum(push[d], axis=0), axis=0, keepdims=True)
            line = ((s * 3 + d) * box_x + bx0) * box_y + by0
            for i in range(local_z):
                within = (lane2 >= i * BOX_Z) & (lane2 < (i + 1) * BOX_Z)
                total = jnp.sum(jnp.where(within, column, 0.0), axis=1, keepdims=True)
                share = share + jnp.where((row_at == line) & (lane_at == bz0 + i), total, 0.0)

    reduced = []
    for axis, (buffer, sem) in enumerate(
        ((force_x, frecv_x), (force_y, frecv_y), (force_z, frecv_z))
    ):
        force_own[axis] = share
        sent = []
        for step in range(1, counts[axis]):
            c = tuple(step if a == axis else 0 for a in range(3))
            copy = pltpu.make_async_remote_copy(
                src_ref=force_own.at[axis],
                dst_ref=buffer.at[me[axis]],
                send_sem=fsend_sem.at[axis, step],
                recv_sem=sem.at[me[axis]],
                device_id=neighbour(c, counts, me),
                device_id_type=MESH,
            )
            copy.start()
            sent.append(copy)
        if axis == 0:
            for q in range(19):
                fine_out[q] = jnp.where(replaced2, refilled(refill2, q), fine_b[q])
        buffer[me[axis]] = share
        for step in range(1, counts[axis]):
            c = tuple(step if a == axis else 0 for a in range(3))
            source = neighbour(c, counts, me)
            pltpu.make_async_remote_copy(
                src_ref=force_own.at[axis],
                dst_ref=buffer.at[source[axis]],
                send_sem=fsend_sem.at[axis, step],
                recv_sem=sem.at[source[axis]],
                device_id=source,
                device_id_type=MESH,
            ).wait_recv()
        reduced += sent
        share = buffer[0]
        for i in range(1, counts[axis]):
            share = share + buffer[i]
    for s in range(2):
        for d in range(3):
            for bx in range(box_x):
                for by in range(box_y):
                    line = ((s * 3 + d) * box_x + bx) * box_y + by
                    force_out[s, d, bx, by : by + 1, :] = share[line : line + 1, 0:box_z]
    for copy in sends2 + reduced:
        copy.wait_send()


def shards(counts, coarse_pdfs, fine_pdfs, centers, sphere_velocity):
    own_x, own_y, own_z = fine_pdfs.shape[1:]
    assert (own_x, own_y, own_z) == (4, SUB, LANES)
    assert own_z % BOX_Z == 0 and BOX_XY % own_y == 0 and BOX_XY % own_x == 0
    boxes = centers.shape[2:]
    f32 = jnp.float32
    lines = -(-6 * boxes[0] * boxes[1] // SUB) * SUB

    def halo_scratch(x, y, z):
        return [
            pltpu.VMEM((2, x, SUB, LANES), f32),
            pltpu.VMEM((2, y, 1, LANES), f32),
            pltpu.VMEM((2, z, SUB, LANES), f32),
            pltpu.VMEM((2, x, SUB, LANES), f32),
            pltpu.VMEM((2, y, 1, LANES), f32),
            pltpu.VMEM((2, z, SUB, LANES), f32),
            pltpu.VMEM((4, FIRST_ROW, 1, LANES), f32),
            pltpu.VMEM((4, z, SUB, LANES), f32),
            pltpu.VMEM((4, z, SUB, LANES), f32),
        ]

    vmem = pl.BlockSpec(memory_space=pltpu.VMEM)
    smem = pl.BlockSpec(memory_space=pltpu.SMEM)
    return pl.pallas_call(
        functools.partial(kernel, counts),
        out_shape=(
            jax.ShapeDtypeStruct(coarse_pdfs.shape, f32),
            jax.ShapeDtypeStruct(fine_pdfs.shape, f32),
            jax.ShapeDtypeStruct((2, 3) + boxes, f32),
        ),
        in_specs=[vmem, vmem, smem, smem],
        out_specs=(vmem, vmem, vmem),
        scratch_shapes=[
            pltpu.VMEM((19, own_x, SUB, LANES), f32),
            pltpu.VMEM((19, own_x, SUB, LANES), f32),
            pltpu.VMEM((19, own_x, SUB, LANES), f32),
        ]
        + halo_scratch(11, ROWS, 2)
        + halo_scratch(6, COARSE_ROW, 1)
        + [
            pltpu.VMEM((2, 18, own_x, SUB, LANES), f32),
            pltpu.VMEM((2, 18, own_x, SUB, LANES), f32),
            pltpu.VMEM((3, own_x, SUB, LANES), f32),
            pltpu.VMEM((2, own_x, SUB, LANES), f32),
            pltpu.VMEM((12, SUB, LANES), f32),
            pltpu.VMEM((3, lines, LANES), f32),
            pltpu.VMEM((counts[0], lines, LANES), f32),
            pltpu.VMEM((counts[1], lines, LANES), f32),
            pltpu.VMEM((counts[2], lines, LANES), f32),
            pltpu.SemaphoreType.DMA((2, 18)),
            pltpu.SemaphoreType.DMA((2, 18)),
            pltpu.SemaphoreType.DMA((3, max(counts))),
            pltpu.SemaphoreType.DMA((counts[0],)),
            pltpu.SemaphoreType.DMA((counts[1],)),
            pltpu.SemaphoreType.DMA((counts[2],)),
        ],
        compiler_params=pltpu.CompilerParams(collective_id=0, has_side_effects=True),
    )(coarse_pdfs, fine_pdfs, centers, sphere_velocity)


def solution(mesh):
    counts = tuple(mesh.shape[a] for a in AXES)
    spec = P(None, "gx", "gy", "gz")
    return jax.shard_map(
        functools.partial(shards, counts),
        mesh=mesh,
        in_specs=(spec, spec, P(), P()),
        out_specs=(spec, spec, P()),
        check_vma=False,
    )
```

```python
import functools

import jax
import jax.numpy as jnp
from jax import lax
from jax.experimental import pallas as pl
from jax.experimental.pallas import tpu as pltpu
from jax.sharding import PartitionSpec as P

BOX_XY = 16
BOX_Z = 64
RADIUS = 4
VELOCITIES = (
    (0, 0, 0),
    (1, 0, 0),
    (-1, 0, 0),
    (0, 1, 0),
    (0, -1, 0),
    (0, 0, 1),
    (0, 0, -1),
    (1, 1, 0),
    (-1, -1, 0),
    (1, -1, 0),
    (-1, 1, 0),
    (1, 0, 1),
    (-1, 0, -1),
    (1, 0, -1),
    (-1, 0, 1),
    (0, 1, 1),
    (0, -1, -1),
    (0, 1, -1),
    (0, -1, 1),
)
OPPOSITE = (0, 2, 1, 4, 3, 6, 5, 8, 7, 10, 9, 12, 11, 14, 13, 16, 15, 18, 17)
WEIGHTS = (1.0 / 3.0,) + (1.0 / 18.0,) * 6 + (1.0 / 36.0,) * 12
COARSE_RATE = 1.25
FINE_RATE = 1.0 / 1.1
HIGHEST = lax.Precision.HIGHEST
MESH = pl.DeviceIdType.MESH
AXES = ("gx", "gy", "gz")
DIRS = VELOCITIES[1:]
RHO = 5
MOVERS = {
    (axis, sign): tuple(q for q in range(19) if VELOCITIES[q][axis] == sign)
    for axis in range(3)
    for sign in (1, -1)
}
SLOT = {1: 0, -1: 1}
PAIRS = ((1, 1), (1, -1), (-1, 1), (-1, -1))
PAIR_SLOT = {pair: i for i, pair in enumerate(PAIRS)}
FIRST_ROW = 8
COARSE_ROW = 32
ROWS = 52
LANES = 128
SUB = 8
VMEM_GRANT = 24 * 1024 * 1024


def iota(shape, axis):
    return lax.broadcasted_iota(jnp.int32, shape, axis)


def project(vectors, direction):
    total = None
    for dim in range(3):
        sign = VELOCITIES[direction][dim]
        if sign == 1:
            total = vectors[dim] if total is None else total + vectors[dim]
        elif sign == -1:
            total = -vectors[dim] if total is None else total - vectors[dim]
    return total


def collide(read, write, rate):
    density = read(0)
    momentum = [None, None, None]
    for q in range(1, 19):
        value = read(q)
        density = density + value
        for dim in range(3):
            sign = VELOCITIES[q][dim]
            if sign:
                if momentum[dim] is None:
                    momentum[dim] = value if sign == 1 else -value
                else:
                    momentum[dim] = momentum[dim] + value if sign == 1 else momentum[dim] - value
    inverse = 1.0 / density
    velocity = [m * inverse for m in momentum]
    base = 1.0 - 1.5 * (
        velocity[0] * velocity[0] + velocity[1] * velocity[1] + velocity[2] * velocity[2]
    )
    scaled = {w: (rate * w) * density for w in set(WEIGHTS)}
    keep = 1.0 - rate
    write(0, keep * read(0) + scaled[WEIGHTS[0]] * base)
    for q in range(1, 19, 2):
        along = project(velocity, q)
        even = base + 4.5 * along * along
        odd = 3.0 * along
        weight = scaled[WEIGHTS[q]]
        write(q, keep * read(q) + weight * (even + odd))
        write(q + 1, keep * read(q + 1) + weight * (even - odd))
    return density


class Halo:
    def __init__(self, send, recv):
        self.sx, self.sy, self.sz = send
        self.rx, self.ry, self.rz, self.rxy, self.rxz, self.ryz = recv

    def pack(self, own, edge_planes, with_rho, rows, lanes, part):
        x0 = 0 if part == 0 else 6
        y0 = FIRST_ROW if part == 0 else COARSE_ROW
        lane = iota((SUB, LANES), 1)
        for sign in (1, -1):
            for k, q in enumerate(MOVERS[0, sign] + ((RHO + 100,) if with_rho else ())):
                self.sx[SLOT[sign], x0 + k] = edge_planes[sign](q)
        for sign in (1, -1):
            row = rows - 1 if sign == 1 else 0
            out = SLOT[sign]
            for k, q in enumerate(MOVERS[1, sign] + ((RHO + 100,) if with_rho else ())):
                self.sy[out, y0 + 4 * k : y0 + 4 * k + 4] = own(q)[:, row : row + 1, :]
            for e, xs in enumerate((1, -1)):
                q = VELOCITIES.index((xs, sign, 0))
                if part == 0:
                    self.sy[out, 2 * e] = edge_planes[xs](q)[row : row + 1, :]
                    self.sy[out, 2 * e + 1] = edge_planes[xs](RHO + 100)[row : row + 1, :]
                else:
                    self.sy[out, 4 + e] = edge_planes[xs](q)[row : row + 1, :]
        for sign in (1, -1):
            source = lanes - 1 if sign == 1 else 0
            packed = jnp.zeros((SUB, LANES), jnp.float32)
            for k, q in enumerate(MOVERS[2, sign] + ((RHO + 100,) if with_rho else ())):
                value = own(q)
                for j in range(4):
                    place = k * 6 + j + 1
                    moved = pltpu.roll(value[j], (place - source) % LANES, 1)
                    packed = jnp.where(lane == place, moved, packed)
                for xs, place in ((1, k * 6 + 5), (-1, k * 6)):
                    if q == RHO + 100 or VELOCITIES[q][0] == xs:
                        moved = pltpu.roll(edge_planes[xs](q), (place - source) % LANES, 1)
                        packed = jnp.where(lane == place, moved, packed)
            self.sz[SLOT[sign], part] = packed

    def pull(self, own, c, q, rows, lanes, part):
        cx, cy, cz = c
        is_rho = q == RHO + 100
        x0 = 0 if part == 0 else 6
        y0 = FIRST_ROW if part == 0 else COARSE_ROW

        def index(axis, sign):
            return RHO if is_rho else MOVERS[axis, sign].index(q)

        def along_x(inner, halo):
            if cx == 1:
                return jnp.concatenate([halo, inner[:3]], axis=0)
            return jnp.concatenate([inner[1:], halo], axis=0)

        value = own
        row = iota((1, SUB, 1), 1)
        if cx:
            value = along_x(own, self.rx[SLOT[cx], x0 + index(0, cx)][None])
        if cy:
            edge = 0 if cy == 1 else rows - 1
            k = y0 + 4 * index(1, cy)
            lines = self.ry[SLOT[cy], k : k + 4]
            if cx:
                e = 0 if cx == 1 else 1
                at = (2 * e + (1 if is_rho else 0)) if part == 0 else 4 + e
                lines = along_x(lines, self.rxy[PAIR_SLOT[cx, cy], at : at + 1])
            value = jnp.where(row == edge, lines, pltpu.roll(value, cy % SUB, 1))
        if cz:
            edge = 0 if cz == 1 else lanes - 1
            k = index(2, cz) * 6
            packed = self.rz[SLOT[cz], part]
            if cy:
                source_row = rows - 1 if cy == 1 else 0
                other = self.ryz[PAIR_SLOT[cy, cz], part][source_row : source_row + 1, :]
                edge_row = 0 if cy == 1 else rows - 1
                packed = jnp.where(
                    iota((SUB, 1), 0) == edge_row, other, pltpu.roll(packed, cy % SUB, 0)
                )
            columns = []
            for ix in range(4):
                j = ix - cx
                if 0 <= j < 4:
                    columns.append(pltpu.roll(packed, (edge - (k + j + 1)) % LANES, 1))
                else:
                    other = self.rxz[PAIR_SLOT[cx, cz], part]
                    place = k + 5 if cx == 1 else k
                    columns.append(pltpu.roll(other, (edge - place) % LANES, 1))
            columns = jnp.stack(columns)
            lane = iota((1, 1, LANES), 2)
            value = jnp.where(lane == edge, columns, pltpu.roll(value, cz % LANES, 2))
        return value


def neighbour(c, counts, me):
    return tuple(lax.rem(me[a] + c[a] + counts[a], counts[a]) for a in range(3))


def kernel(
    counts,
    coarse_hbm,
    fine_hbm,
    centers_hbm,
    speeds_hbm,
    coarse_res,
    fine_res,
    force_res,
    coarse_in,
    fine_in,
    centers,
    speeds,
    coarse_out,
    force_out,
    local_sem,
    fine_a,
    fine_b,
    coarse,
    sx1,
    sy1,
    sz1,
    rx1,
    ry1,
    rz1,
    rxy1,
    rxz1,
    ryz1,
    sx2,
    sy2,
    sz2,
    rx2,
    ry2,
    rz2,
    rxy2,
    rxz2,
    ryz2,
    opens,
    news,
    own_masks,
    dens,
    fill_ref,
    force_own,
    send_sem,
    recv_sem,
    *force_parts,
):
    me = tuple(lax.axis_index(a) for a in AXES)
    own_x, own_y, own_z = fine_in.shape[1], fine_in.shape[2], fine_in.shape[3]
    rows_c, lanes_c = coarse_in.shape[2], coarse_in.shape[3]
    total_x = own_x * counts[0]
    box_x, box_y, box_z = centers.shape[2], centers.shape[3], centers.shape[4]
    local_z = own_z // BOX_Z

    barrier = pltpu.get_barrier_semaphore()
    for c in DIRS:
        pl.semaphore_signal(
            barrier, inc=1, device_id=neighbour(c, counts, me), device_id_type=MESH
        )
    phases = force_phases(counts)
    for phase in phases:
        for c in group_steps(phase, counts):
            pl.semaphore_signal(
                barrier, inc=1, device_id=neighbour(c, counts, me), device_id_type=MESH
            )
    loads = [
        pltpu.make_async_copy(src, dst, local_sem.at[i])
        for i, (src, dst) in enumerate(
            (
                (fine_hbm, fine_in),
                (coarse_hbm, coarse_in),
                (centers_hbm, centers),
                (speeds_hbm, speeds),
            )
        )
    ]
    for copy in loads:
        copy.start()
    loads[0].wait()

    def write_a(q, value):
        fine_a[q] = value

    rho = collide(lambda q: fine_in[q], write_a, FINE_RATE)
    coarse[...] = jnp.ones(coarse.shape, jnp.float32)
    loads[1].wait()
    coarse[:, :, 0:rows_c, 0:lanes_c] = coarse_in[...]

    def write_c(q, value):
        coarse[q] = value

    rho_c = collide(lambda q: coarse[q], write_c, COARSE_RATE)
    first = me[0] == 0
    last = me[0] == counts[0] - 1
    row3 = iota((1, SUB, 1), 1)

    planes = []
    for sign, ix in ((1, 3), (-1, 0)):
        planes += [coarse[q, ix] for q in MOVERS[0, sign]] + [rho_c[ix]]
    grow = (iota((LANES, LANES), 0) == (iota((LANES, LANES), 1) >> 1)).astype(jnp.float32)
    wide = jnp.dot(
        jnp.concatenate(planes, axis=0), grow, precision=HIGHEST, preferred_element_type=jnp.float32
    ).reshape(12, SUB, LANES)
    tall = wide[:, 3:4, :]
    for r in (2, 1, 0):
        tall = jnp.where(row3 < 2 * r + 2, wide[:, r : r + 1, :], tall)
    fill_ref[...] = tall

    planes = []
    for sign, ix in ((1, 3), (-1, 0)):
        for q in MOVERS[0, sign]:
            plane = fine_a[q, ix]
            planes.append(plane + pltpu.roll(plane, SUB - 1, 0))
    shrink = 0.25 * ((iota((LANES, LANES), 0) >> 1) == iota((LANES, LANES), 1)).astype(jnp.float32)
    thin = jnp.dot(
        jnp.concatenate(planes, axis=0),
        shrink,
        precision=HIGHEST,
        preferred_element_type=jnp.float32,
    ).reshape(10, SUB, LANES)
    flat = thin[:, 6:7, :]
    for r in (2, 1, 0):
        flat = jnp.where(row3 <= r, thin[:, 2 * r : 2 * r + 1, :], flat)

    def fine_edges(ref, density):
        def plane(sign):
            ix, at_end, base = (3, last, 0) if sign == 1 else (0, first, 6)

            def get(q):
                is_rho = q == RHO + 100
                k = RHO if is_rho else MOVERS[0, sign].index(q)
                mine = density[ix] if is_rho else ref[q, ix]
                return jnp.where(at_end, fill_ref[base + k], mine)

            return get

        return {1: plane(1), -1: plane(-1)}

    def coarse_edge(sign):
        ix, at_end, base = (3, last, 0) if sign == 1 else (0, first, 5)

        def get(q):
            return jnp.where(at_end, flat[base + MOVERS[0, sign].index(q)], coarse[q, ix])

        return get

    halo1 = Halo((sx1, sy1, sz1), (rx1, ry1, rz1, rxy1, rxz1, ryz1))
    halo2 = Halo((sx2, sy2, sz2), (rx2, ry2, rz2, rxy2, rxz2, ryz2))
    halo1.pack(
        lambda q: rho if q == RHO + 100 else fine_a[q],
        fine_edges(fine_a, rho),
        True,
        own_y,
        own_z,
        0,
    )
    halo1.pack(
        lambda q: coarse[q],
        {1: coarse_edge(1), -1: coarse_edge(-1)},
        False,
        rows_c,
        lanes_c,
        1,
    )

    def copies(halo, phase):
        made = []
        for i, c in enumerate(DIRS):
            cx, cy, cz = c
            if cz:
                if cx:
                    dst = halo.rxz.at[PAIR_SLOT[cx, cz]]
                elif cy:
                    dst = halo.ryz.at[PAIR_SLOT[cy, cz]]
                else:
                    dst = halo.rz.at[SLOT[cz]]
                src = halo.sz.at[SLOT[cz]]
            elif cy:
                if cx:
                    src = halo.sy.at[SLOT[cy], pl.ds(0, FIRST_ROW)]
                    dst = halo.rxy.at[PAIR_SLOT[cx, cy]]
                else:
                    src = halo.sy.at[SLOT[cy]]
                    dst = halo.ry.at[SLOT[cy]]
            else:
                src = halo.sx.at[SLOT[cx]]
                dst = halo.rx.at[SLOT[cx]]
            made.append(
                pltpu.make_async_remote_copy(
                    src_ref=src,
                    dst_ref=dst,
                    send_sem=send_sem.at[phase, i],
                    recv_sem=recv_sem.at[phase, i],
                    device_id=neighbour(c, counts, me),
                    device_id_type=MESH,
                )
            )
        return made

    pl.semaphore_wait(barrier, 18 + sum(len(group_steps(p, counts)) for p in phases))
    sends1 = copies(halo1, 0)
    for copy in sends1:
        copy.start()

    loads[2].wait()
    loads[3].wait()
    start_x, start_y = me[0] * own_x, me[1] * own_y
    total_y = own_y * counts[1]
    bx0 = lax.div(start_x, BOX_XY)
    by0 = lax.div(start_y, BOX_XY)
    bz0 = me[2] * local_z
    bx_near = {
        1: lax.div(lax.max(start_x - 1, 0), BOX_XY),
        -1: lax.min(lax.div(start_x + own_x, BOX_XY), box_x - 1),
        0: bx0,
    }
    by_near = {
        1: lax.div(lax.rem(start_y + total_y - 1, total_y), BOX_XY),
        -1: lax.div(lax.rem(start_y + own_y, total_y), BOX_XY),
        0: by0,
    }
    bz_all = [lax.rem(bz0 + box_z + i, box_z) for i in range(-1, local_z + 1)]
    lane3 = iota((1, 1, LANES), 2)
    plane3 = iota((own_x, 1, LANES), 0)
    memo = {}

    def along_lanes(get, key, bx_key, by_key, cz):
        full = (key, bx_key, by_key, cz)
        if full in memo:
            return memo[full]
        bx, by = bx_near[bx_key], by_near[by_key]
        at = lane3 - cz
        value = jnp.full((1, 1, LANES), get(bx, by, bz_all[1]))
        for i in range(1, local_z):
            value = jnp.where(at >= i * BOX_Z, get(bx, by, bz_all[1 + i]), value)
        if cz == 1:
            value = jnp.where(at < 0, get(bx, by, bz_all[0]), value)
        elif cz == -1:
            value = jnp.where(at >= own_z, get(bx, by, bz_all[-1]), value)
        value = value.astype(jnp.float32)
        memo[full] = value
        return value

    def box_field(get, key, c):
        cx, cy, cz = c

        def on_rows(bx_key):
            own = along_lanes(get, key, bx_key, 0, cz)
            if cy == 0 or box_y == 1:
                return own
            edge = 0 if cy == 1 else own_y - 1
            return jnp.where(row3 == edge, along_lanes(get, key, bx_key, cy, cz), own)

        if cx == 0 or box_x == 1:
            return on_rows(0)
        edge = 0 if cx == 1 else own_x - 1
        return jnp.where(plane3 == edge, on_rows(cx), on_rows(0))

    def center_getter(moment, dim):
        return lambda bx, by, bz: centers[moment, dim, bx, by, bz]

    def speed_getter(dim):
        return lambda bx, by, bz: speeds[dim, bx, by, bz]

    def speeds_at(c):
        return [box_field(speed_getter(dim), ("u", dim), c) for dim in range(3)]

    def inside_at(cx):
        at = start_x + plane3 - cx
        return (at >= 0) & (at < total_x)

    def solids_at(c):
        cx, cy, cz = c
        off_x = ((start_x + plane3 - cx) & (BOX_XY - 1)).astype(jnp.float32)
        off_y = ((start_y + iota((1, SUB, LANES), 1) - cy) & (BOX_XY - 1)).astype(jnp.float32)
        off_z = ((lane3 - cz) & (BOX_Z - 1)).astype(jnp.float32)
        found = []
        for moment in range(3):
            gap_x = off_x - box_field(center_getter(moment, 0), (moment, 0), c)
            gap_y = off_y - box_field(center_getter(moment, 1), (moment, 1), c)
            gap_z = off_z - box_field(center_getter(moment, 2), (moment, 2), c)
            distance = (gap_x * gap_x + gap_z * gap_z) + gap_y * gap_y
            if cx:
                distance = jnp.where(inside_at(cx), distance, 1e9)
            found.append(jnp.where(distance <= float(RADIUS * RADIUS), 1.0, 0.0))
        return found

    own_solids = solids_at((0, 0, 0))
    for moment in range(3):
        own_masks[moment] = own_solids[moment]
    sums = [jnp.full((own_x, SUB, LANES), WEIGHTS[0], jnp.float32) for s in range(2)]
    for q in range(1, 19):
        s0, s1, s2 = solids_at(VELOCITIES[q])
        for s, (before, after) in enumerate(((s0, s1), (s1, s2))):
            free = (1.0 - before) * (1.0 - after)
            opens[s, q - 1] = free
            news[s, q - 1] = after
            sums[s] = sums[s] + WEIGHTS[q] * free
    for s in range(2):
        dens[s] = sums[s]
    own_speed = speeds_at((0, 0, 0))
    quiet = 1.0 - 1.5 * (
        own_speed[0] * own_speed[0] + own_speed[1] * own_speed[1] + own_speed[2] * own_speed[2]
    )

    def substep(s, halo, ref, density, write):
        covered = own_masks[s + 1] > 0.5
        uncovered = own_masks[s] > 0.5
        push = [jnp.zeros((own_x, SUB, LANES), jnp.float32) for d in range(3)]
        numerator = WEIGHTS[0] * density
        for q in range(1, 19):
            c = VELOCITIES[q]
            near = halo.pull(density, c, RHO + 100, own_y, own_z, 0)
            free = opens[s, q - 1]
            freed = near * free
            numerator = numerator + WEIGHTS[q] * freed
            arrived = halo.pull(ref[q], c, q, own_y, own_z, 0)
            here = (6.0 * WEIGHTS[q]) * project(own_speed, q)
            link = (2.0 * arrived - here * near) * free
            if c[0]:
                link = jnp.where(inside_at(c[0]), link, 0.0)
            for d in range(3):
                if c[d] == 1:
                    push[d] = push[d] + link
                elif c[d] == -1:
                    push[d] = push[d] - link
            wall = (6.0 * WEIGHTS[q]) * project(speeds_at(c), q)
            bounced = ref[OPPOSITE[q]] + density * wall
            arrived = jnp.where(news[s, q - 1] > 0.5, bounced, arrived)
            write(q, jnp.where(covered, ref[q], arrived))
        write(0, ref[0])
        refill = numerator / dens[s]
        replaced = uncovered & jnp.logical_not(covered)
        return refill, replaced, [jnp.where(covered, p, 0.0) for p in push]

    def refilled(refill, q):
        if q == 0:
            return refill * (WEIGHTS[0] * quiet)
        along = project(own_speed, q)
        return refill * (WEIGHTS[q] * (quiet + 3.0 * along + 4.5 * along * along))

    for copy in sends1:
        copy.wait_recv()

    def write_b(q, value):
        fine_b[q] = value

    refill, replaced, push1 = substep(0, halo1, fine_a, rho, write_b)
    for copy in sends1:
        copy.wait_send()

    def middle(q):
        return jnp.where(replaced, refilled(refill, q), fine_b[q])

    rho2 = collide(middle, write_a, FINE_RATE)
    halo2.pack(
        lambda q: rho2 if q == RHO + 100 else fine_a[q],
        fine_edges(fine_a, rho2),
        True,
        own_y,
        own_z,
        0,
    )
    sends2 = copies(halo2, 1)
    for copy in sends2:
        copy.start()

    for q in range(19):
        value = coarse[q]
        if q:
            value = halo1.pull(value, VELOCITIES[q], q, rows_c, lanes_c, 1)
        coarse_out[q] = value[:, 0:rows_c, 0:lanes_c]
    stores = [pltpu.make_async_copy(coarse_out, coarse_res, local_sem.at[4])]
    stores[0].start()

    for copy in sends2:
        copy.wait_recv()

    def write_b2(q, value):
        fine_b[q] = value

    refill2, replaced2, push2 = substep(1, halo2, fine_a, rho2, write_b2)

    shape = force_own.shape[1:]
    flat_at = iota(shape, 0) * LANES + iota(shape, 1)
    share = jnp.zeros(shape, jnp.float32)
    lane2 = iota((1, LANES), 1)
    for s, push in enumerate((push1, push2)):
        for d in range(3):
            column = jnp.sum(jnp.sum(push[d], axis=0), axis=0, keepdims=True)
            line = ((s * 3 + d) * box_x + bx0) * box_y + by0
            for i in range(local_z):
                within = (lane2 >= i * BOX_Z) & (lane2 < (i + 1) * BOX_Z)
                total = jnp.sum(jnp.where(within, column, 0.0), axis=1, keepdims=True)
                share = share + jnp.where(flat_at == line * box_z + bz0 + i, total, 0.0)

    reduced = []
    for number, phase in enumerate(phases):
        buffer, out_sem, in_sem = force_parts[3 * number : 3 * number + 3]
        steps = group_steps(phase, counts)
        rank = group_rank(phase, counts, me)
        force_own[number] = share
        for i, c in enumerate(steps):
            copy = pltpu.make_async_remote_copy(
                src_ref=force_own.at[number],
                dst_ref=buffer.at[rank],
                send_sem=out_sem.at[i],
                recv_sem=in_sem.at[rank],
                device_id=neighbour(c, counts, me),
                device_id_type=MESH,
            )
            copy.start()
            reduced.append(copy)
        if number == 0:
            for q in range(19):
                fine_b[q] = jnp.where(replaced2, refilled(refill2, q), fine_b[q])
            stores.append(pltpu.make_async_copy(fine_b, fine_res, local_sem.at[5]))
            stores[1].start()
        buffer[rank] = share
        for i, c in enumerate(steps):
            source = neighbour(c, counts, me)
            at = group_rank(phase, counts, source)
            pltpu.make_async_remote_copy(
                src_ref=force_own.at[number],
                dst_ref=buffer.at[at],
                send_sem=out_sem.at[i],
                recv_sem=in_sem.at[at],
                device_id=source,
                device_id_type=MESH,
            ).wait_recv()
        share = jnp.sum(buffer[...], axis=0)
    for s in range(2):
        for d in range(3):
            for bx in range(box_x):
                for by in range(box_y):
                    first_at = (((s * 3 + d) * box_x + bx) * box_y + by) * box_z
                    moved = pltpu.roll(share, -first_at % LANES, 1)
                    line = first_at // LANES
                    force_out[s, d, bx, by : by + 1, :] = moved[line : line + 1, 0:box_z]
    stores.append(pltpu.make_async_copy(force_out, force_res, local_sem.at[6]))
    stores[2].start()
    for copy in sends2 + reduced:
        copy.wait_send()
    for copy in stores:
        copy.wait()


def force_phases(counts):
    if counts[0] * counts[1] * counts[2] <= 64:
        return ((0, 1, 2),)
    return ((0,), (1,), (2,))


def group_steps(phase, counts):
    spans = [range(counts[a]) if a in phase else range(1) for a in range(3)]
    steps = [(x, y, z) for x in spans[0] for y in spans[1] for z in spans[2]]
    return steps[1:]


def group_rank(phase, counts, at):
    rank = 0
    for a in phase:
        rank = rank * counts[a] + at[a]
    return rank


def finish(*refs):
    n = len(refs) // 2
    sem = refs[2 * n]
    outs = [pltpu.make_async_copy(refs[i], refs[n + i], sem.at[i]) for i in range(n)]
    for copy in outs:
        copy.start()
    for copy in outs:
        copy.wait()


def shards(counts, coarse_pdfs, fine_pdfs, centers, sphere_velocity):
    own_x, own_y, own_z = fine_pdfs.shape[1:]
    assert (own_x, own_y, own_z) == (4, SUB, LANES)
    assert own_z % BOX_Z == 0 and BOX_XY % own_y == 0 and BOX_XY % own_x == 0
    boxes = centers.shape[2:]
    f32 = jnp.float32
    lines = -(-6 * boxes[0] * boxes[1] * boxes[2] // LANES)
    lines = lines if lines == 1 else -(-lines // SUB) * SUB
    assert LANES % boxes[2] == 0
    phases = force_phases(counts)
    force_scratch = []
    for phase in phases:
        size = len(group_steps(phase, counts)) + 1
        force_scratch += [
            pltpu.VMEM((size, lines, LANES), f32),
            pltpu.SemaphoreType.DMA((size - 1,)),
            pltpu.SemaphoreType.DMA((size,)),
        ]

    def halo_scratch(x, y, z):
        return [
            pltpu.VMEM((2, x, SUB, LANES), f32),
            pltpu.VMEM((2, y, 1, LANES), f32),
            pltpu.VMEM((2, z, SUB, LANES), f32),
            pltpu.VMEM((2, x, SUB, LANES), f32),
            pltpu.VMEM((2, y, 1, LANES), f32),
            pltpu.VMEM((2, z, SUB, LANES), f32),
            pltpu.VMEM((4, FIRST_ROW, 1, LANES), f32),
            pltpu.VMEM((4, z, SUB, LANES), f32),
            pltpu.VMEM((4, z, SUB, LANES), f32),
        ]

    anywhere = pl.BlockSpec(memory_space=pl.ANY)
    out_shape = (
        jax.ShapeDtypeStruct(coarse_pdfs.shape, f32),
        jax.ShapeDtypeStruct(fine_pdfs.shape, f32),
        jax.ShapeDtypeStruct((2, 3) + boxes, f32),
    )
    results = pl.pallas_call(
        functools.partial(kernel, counts),
        out_shape=out_shape,
        in_specs=[pl.BlockSpec(memory_space=pltpu.HBM)] * 4,
        out_specs=(anywhere,) * 3,
        scratch_shapes=[
            pltpu.VMEM(coarse_pdfs.shape, f32),
            pltpu.VMEM(fine_pdfs.shape, f32),
            pltpu.SMEM(centers.shape, jnp.int32),
            pltpu.SMEM(sphere_velocity.shape, f32),
            pltpu.VMEM(coarse_pdfs.shape, f32),
            pltpu.VMEM((2, 3) + boxes, f32),
            pltpu.SemaphoreType.DMA((7,)),
            pltpu.VMEM((19, own_x, SUB, LANES), f32),
            pltpu.VMEM((19, own_x, SUB, LANES), f32),
            pltpu.VMEM((19, own_x, SUB, LANES), f32),
        ]
        + halo_scratch(11, ROWS, 2)
        + halo_scratch(6, COARSE_ROW, 1)
        + [
            pltpu.VMEM((2, 18, own_x, SUB, LANES), f32),
            pltpu.VMEM((2, 18, own_x, SUB, LANES), f32),
            pltpu.VMEM((3, own_x, SUB, LANES), f32),
            pltpu.VMEM((2, own_x, SUB, LANES), f32),
            pltpu.VMEM((12, SUB, LANES), f32),
            pltpu.VMEM((len(phases), lines, LANES), f32),
            pltpu.SemaphoreType.DMA((2, 18)),
            pltpu.SemaphoreType.DMA((2, 18)),
        ]
        + force_scratch,
        compiler_params=pltpu.CompilerParams(
            collective_id=0, has_side_effects=True, vmem_limit_bytes=VMEM_GRANT
        ),
    )(coarse_pdfs, fine_pdfs, centers, sphere_velocity)
    return pl.pallas_call(
        finish,
        out_shape=out_shape,
        in_specs=[anywhere] * 3,
        out_specs=(anywhere,) * 3,
        scratch_shapes=[pltpu.SemaphoreType.DMA((3,))],
        compiler_params=pltpu.CompilerParams(vmem_limit_bytes=VMEM_GRANT),
    )(*results)


def solution(mesh):
    counts = tuple(mesh.shape[a] for a in AXES)
    spec = P(None, "gx", "gy", "gz")
    return jax.shard_map(
        functools.partial(shards, counts),
        mesh=mesh,
        in_specs=(spec, spec, P(), P()),
        out_specs=(spec, spec, P()),
        check_vma=False,
    )
```

```python
import functools

import jax
import jax.numpy as jnp
from jax import lax
from jax.experimental import pallas as pl
from jax.experimental.pallas import tpu as pltpu
from jax.sharding import PartitionSpec as P

BOX_XY = 16
BOX_Z = 64
RADIUS = 4
VELOCITIES = (
    (0, 0, 0),
    (1, 0, 0),
    (-1, 0, 0),
    (0, 1, 0),
    (0, -1, 0),
    (0, 0, 1),
    (0, 0, -1),
    (1, 1, 0),
    (-1, -1, 0),
    (1, -1, 0),
    (-1, 1, 0),
    (1, 0, 1),
    (-1, 0, -1),
    (1, 0, -1),
    (-1, 0, 1),
    (0, 1, 1),
    (0, -1, -1),
    (0, 1, -1),
    (0, -1, 1),
)
OPPOSITE = (0, 2, 1, 4, 3, 6, 5, 8, 7, 10, 9, 12, 11, 14, 13, 16, 15, 18, 17)
WEIGHTS = (1.0 / 3.0,) + (1.0 / 18.0,) * 6 + (1.0 / 36.0,) * 12
COARSE_RATE = 1.25
FINE_RATE = 1.0 / 1.1
HIGHEST = lax.Precision.HIGHEST
MESH = pl.DeviceIdType.MESH
AXES = ("gx", "gy", "gz")
DIRS = VELOCITIES[1:]
RHO = 5
MOVERS = {
    (axis, sign): tuple(q for q in range(19) if VELOCITIES[q][axis] == sign)
    for axis in range(3)
    for sign in (1, -1)
}
SLOT = {1: 0, -1: 1}
PAIRS = ((1, 1), (1, -1), (-1, 1), (-1, -1))
PAIR_SLOT = {pair: i for i, pair in enumerate(PAIRS)}
FIRST_ROW = 8
COARSE_ROW = 32
ROWS = 52
LANES = 128
SUB = 8
VMEM_GRANT = 24 * 1024 * 1024


def iota(shape, axis):
    return lax.broadcasted_iota(jnp.int32, shape, axis)


def project(vectors, direction):
    total = None
    for dim in range(3):
        sign = VELOCITIES[direction][dim]
        if sign == 1:
            total = vectors[dim] if total is None else total + vectors[dim]
        elif sign == -1:
            total = -vectors[dim] if total is None else total - vectors[dim]
    return total


def collide(read, write, rate):
    density = read(0)
    momentum = [None, None, None]
    for q in range(1, 19):
        value = read(q)
        density = density + value
        for dim in range(3):
            sign = VELOCITIES[q][dim]
            if sign:
                if momentum[dim] is None:
                    momentum[dim] = value if sign == 1 else -value
                else:
                    momentum[dim] = momentum[dim] + value if sign == 1 else momentum[dim] - value
    inverse = 1.0 / density
    velocity = [m * inverse for m in momentum]
    base = 1.0 - 1.5 * (
        velocity[0] * velocity[0] + velocity[1] * velocity[1] + velocity[2] * velocity[2]
    )
    scaled = {w: (rate * w) * density for w in set(WEIGHTS)}
    keep = 1.0 - rate
    write(0, keep * read(0) + scaled[WEIGHTS[0]] * base)
    for q in range(1, 19, 2):
        along = project(velocity, q)
        even = base + 4.5 * along * along
        odd = 3.0 * along
        weight = scaled[WEIGHTS[q]]
        write(q, keep * read(q) + weight * (even + odd))
        write(q + 1, keep * read(q + 1) + weight * (even - odd))
    return density


class Halo:
    def __init__(self, send, recv):
        self.sx, self.sy, self.sz = send
        self.rx, self.ry, self.rz, self.rxy, self.rxz, self.ryz = recv

    def pack(self, own, edge_planes, with_rho, rows, lanes, part):
        x0 = 0 if part == 0 else 6
        y0 = FIRST_ROW if part == 0 else COARSE_ROW
        lane = iota((SUB, LANES), 1)
        for sign in (1, -1):
            for k, q in enumerate(MOVERS[0, sign] + ((RHO + 100,) if with_rho else ())):
                self.sx[SLOT[sign], x0 + k] = edge_planes[sign](q)
        for sign in (1, -1):
            row = rows - 1 if sign == 1 else 0
            out = SLOT[sign]
            for k, q in enumerate(MOVERS[1, sign] + ((RHO + 100,) if with_rho else ())):
                self.sy[out, y0 + 4 * k : y0 + 4 * k + 4] = own(q)[:, row : row + 1, :]
            for e, xs in enumerate((1, -1)):
                q = VELOCITIES.index((xs, sign, 0))
                if part == 0:
                    self.sy[out, 2 * e] = edge_planes[xs](q)[row : row + 1, :]
                    self.sy[out, 2 * e + 1] = edge_planes[xs](RHO + 100)[row : row + 1, :]
                else:
                    self.sy[out, 4 + e] = edge_planes[xs](q)[row : row + 1, :]
        for sign in (1, -1):
            source = lanes - 1 if sign == 1 else 0
            packed = jnp.zeros((SUB, LANES), jnp.float32)
            for k, q in enumerate(MOVERS[2, sign] + ((RHO + 100,) if with_rho else ())):
                value = own(q)
                for j in range(4):
                    place = k * 6 + j + 1
                    moved = pltpu.roll(value[j], (place - source) % LANES, 1)
                    packed = jnp.where(lane == place, moved, packed)
                for xs, place in ((1, k * 6 + 5), (-1, k * 6)):
                    if q == RHO + 100 or VELOCITIES[q][0] == xs:
                        moved = pltpu.roll(edge_planes[xs](q), (place - source) % LANES, 1)
                        packed = jnp.where(lane == place, moved, packed)
            self.sz[SLOT[sign], part] = packed

    def pull(self, own, c, q, rows, lanes, part):
        cx, cy, cz = c
        is_rho = q == RHO + 100
        x0 = 0 if part == 0 else 6
        y0 = FIRST_ROW if part == 0 else COARSE_ROW

        def index(axis, sign):
            return RHO if is_rho else MOVERS[axis, sign].index(q)

        def along_x(inner, halo):
            if cx == 1:
                return jnp.concatenate([halo, inner[:3]], axis=0)
            return jnp.concatenate([inner[1:], halo], axis=0)

        value = own
        row = iota((1, SUB, 1), 1)
        if cx:
            value = along_x(own, self.rx[SLOT[cx], x0 + index(0, cx)][None])
        if cy:
            edge = 0 if cy == 1 else rows - 1
            k = y0 + 4 * index(1, cy)
            lines = self.ry[SLOT[cy], k : k + 4]
            if cx:
                e = 0 if cx == 1 else 1
                at = (2 * e + (1 if is_rho else 0)) if part == 0 else 4 + e
                lines = along_x(lines, self.rxy[PAIR_SLOT[cx, cy], at : at + 1])
            value = jnp.where(row == edge, lines, pltpu.roll(value, cy % SUB, 1))
        if cz:
            edge = 0 if cz == 1 else lanes - 1
            k = index(2, cz) * 6
            packed = self.rz[SLOT[cz], part]
            if cy:
                source_row = rows - 1 if cy == 1 else 0
                other = self.ryz[PAIR_SLOT[cy, cz], part][source_row : source_row + 1, :]
                edge_row = 0 if cy == 1 else rows - 1
                packed = jnp.where(
                    iota((SUB, 1), 0) == edge_row, other, pltpu.roll(packed, cy % SUB, 0)
                )
            columns = []
            for ix in range(4):
                j = ix - cx
                if 0 <= j < 4:
                    columns.append(pltpu.roll(packed, (edge - (k + j + 1)) % LANES, 1))
                else:
                    other = self.rxz[PAIR_SLOT[cx, cz], part]
                    place = k + 5 if cx == 1 else k
                    columns.append(pltpu.roll(other, (edge - place) % LANES, 1))
            columns = jnp.stack(columns)
            lane = iota((1, 1, LANES), 2)
            value = jnp.where(lane == edge, columns, pltpu.roll(value, cz % LANES, 2))
        return value


def neighbour(c, counts, me):
    return tuple(lax.rem(me[a] + c[a] + counts[a], counts[a]) for a in range(3))


def kernel(
    counts,
    coarse_hbm,
    fine_hbm,
    centers_hbm,
    speeds_hbm,
    coarse_res,
    fine_res,
    force_res,
    coarse_in,
    fine_in,
    centers,
    speeds,
    coarse_out,
    force_out,
    local_sem,
    fine_a,
    fine_b,
    coarse,
    sx1,
    sy1,
    sz1,
    rx1,
    ry1,
    rz1,
    rxy1,
    rxz1,
    ryz1,
    sx2,
    sy2,
    sz2,
    rx2,
    ry2,
    rz2,
    rxy2,
    rxz2,
    ryz2,
    opens,
    news,
    own_masks,
    dens,
    fill_ref,
    force_own,
    send_sem,
    recv_sem,
    *force_parts,
):
    me = tuple(lax.axis_index(a) for a in AXES)
    own_x, own_y, own_z = fine_in.shape[1], fine_in.shape[2], fine_in.shape[3]
    rows_c, lanes_c = coarse_in.shape[2], coarse_in.shape[3]
    total_x = own_x * counts[0]
    box_x, box_y, box_z = centers.shape[2], centers.shape[3], centers.shape[4]
    local_z = own_z // BOX_Z

    barrier = pltpu.get_barrier_semaphore()
    for c in DIRS:
        pl.semaphore_signal(
            barrier, inc=1, device_id=neighbour(c, counts, me), device_id_type=MESH
        )
    phases = force_phases(counts)
    for phase in phases:
        for c in group_steps(phase, counts):
            pl.semaphore_signal(
                barrier, inc=1, device_id=neighbour(c, counts, me), device_id_type=MESH
            )
    loads = [
        pltpu.make_async_copy(src, dst, local_sem.at[i])
        for i, (src, dst) in enumerate(
            (
                (fine_hbm, fine_in),
                (coarse_hbm, coarse_in),
                (centers_hbm, centers),
                (speeds_hbm, speeds),
            )
        )
    ]
    for copy in loads:
        copy.start()
    loads[0].wait()

    def write_a(q, value):
        fine_a[q] = value

    rho = collide(lambda q: fine_in[q], write_a, FINE_RATE)
    coarse[...] = jnp.ones(coarse.shape, jnp.float32)
    loads[1].wait()
    coarse[:, :, 0:rows_c, 0:lanes_c] = coarse_in[...]

    def write_c(q, value):
        coarse[q] = value

    rho_c = collide(lambda q: coarse[q], write_c, COARSE_RATE)
    first = me[0] == 0
    last = me[0] == counts[0] - 1
    row3 = iota((1, SUB, 1), 1)

    planes = []
    for sign, ix in ((1, 3), (-1, 0)):
        planes += [coarse[q, ix] for q in MOVERS[0, sign]] + [rho_c[ix]]
    grow = (iota((LANES, LANES), 0) == (iota((LANES, LANES), 1) >> 1)).astype(jnp.float32)
    wide = jnp.dot(
        jnp.concatenate(planes, axis=0), grow, precision=HIGHEST, preferred_element_type=jnp.float32
    ).reshape(12, SUB, LANES)
    tall = wide[:, 3:4, :]
    for r in (2, 1, 0):
        tall = jnp.where(row3 < 2 * r + 2, wide[:, r : r + 1, :], tall)
    fill_ref[...] = tall

    def fine_edges(ref, density):
        def plane(sign):
            ix, at_end, base = (3, last, 0) if sign == 1 else (0, first, 6)

            def get(q):
                is_rho = q == RHO + 100
                k = RHO if is_rho else MOVERS[0, sign].index(q)
                mine = density[ix] if is_rho else ref[q, ix]
                return jnp.where(at_end, fill_ref[base + k], mine)

            return get

        return {1: plane(1), -1: plane(-1)}

    halo1 = Halo((sx1, sy1, sz1), (rx1, ry1, rz1, rxy1, rxz1, ryz1))
    halo2 = Halo((sx2, sy2, sz2), (rx2, ry2, rz2, rxy2, rxz2, ryz2))
    halo1.pack(
        lambda q: rho if q == RHO + 100 else fine_a[q],
        fine_edges(fine_a, rho),
        True,
        own_y,
        own_z,
        0,
    )
    def copies(halo, phase):
        coarse_part = phase == 2
        x_part = pl.ds(6, 5) if coarse_part else pl.ds(0, 6)
        y_first, y_last = (COARSE_ROW, ROWS) if coarse_part else (FIRST_ROW, COARSE_ROW)
        y_part = pl.ds(y_first, y_last - y_first)
        edge_part = pl.ds(4, 4) if coarse_part else pl.ds(0, 4)
        z_part = 1 if coarse_part else 0
        made = []
        for i, c in enumerate(DIRS):
            cx, cy, cz = c
            if cz:
                if cx:
                    dst = halo.rxz.at[PAIR_SLOT[cx, cz], z_part]
                elif cy:
                    dst = halo.ryz.at[PAIR_SLOT[cy, cz], z_part]
                else:
                    dst = halo.rz.at[SLOT[cz], z_part]
                src = halo.sz.at[SLOT[cz], z_part]
            elif cy:
                if cx:
                    src = halo.sy.at[SLOT[cy], edge_part]
                    dst = halo.rxy.at[PAIR_SLOT[cx, cy], edge_part]
                else:
                    src = halo.sy.at[SLOT[cy], y_part]
                    dst = halo.ry.at[SLOT[cy], y_part]
            else:
                src = halo.sx.at[SLOT[cx], x_part]
                dst = halo.rx.at[SLOT[cx], x_part]
            made.append(
                pltpu.make_async_remote_copy(
                    src_ref=src,
                    dst_ref=dst,
                    send_sem=send_sem.at[phase, i],
                    recv_sem=recv_sem.at[phase, i],
                    device_id=neighbour(c, counts, me),
                    device_id_type=MESH,
                )
            )
        return made

    pl.semaphore_wait(barrier, 18 + sum(len(group_steps(p, counts)) for p in phases))
    sends1 = copies(halo1, 0)
    for copy in reversed(sends1):
        copy.start()

    planes = []
    for sign, ix in ((1, 3), (-1, 0)):
        for q in MOVERS[0, sign]:
            plane = fine_a[q, ix]
            planes.append(plane + pltpu.roll(plane, SUB - 1, 0))
    shrink = 0.25 * ((iota((LANES, LANES), 0) >> 1) == iota((LANES, LANES), 1)).astype(jnp.float32)
    thin = jnp.dot(
        jnp.concatenate(planes, axis=0),
        shrink,
        precision=HIGHEST,
        preferred_element_type=jnp.float32,
    ).reshape(10, SUB, LANES)
    flat = thin[:, 6:7, :]
    for r in (2, 1, 0):
        flat = jnp.where(row3 <= r, thin[:, 2 * r : 2 * r + 1, :], flat)

    def coarse_edge(sign):
        ix, at_end, base = (3, last, 0) if sign == 1 else (0, first, 5)

        def get(q):
            return jnp.where(at_end, flat[base + MOVERS[0, sign].index(q)], coarse[q, ix])

        return get

    halo1.pack(
        lambda q: coarse[q],
        {1: coarse_edge(1), -1: coarse_edge(-1)},
        False,
        rows_c,
        lanes_c,
        1,
    )

    sends_c = copies(halo1, 2)
    for copy in reversed(sends_c):
        copy.start()

    loads[2].wait()
    loads[3].wait()
    start_x, start_y = me[0] * own_x, me[1] * own_y
    total_y = own_y * counts[1]
    bx0 = lax.div(start_x, BOX_XY)
    by0 = lax.div(start_y, BOX_XY)
    bz0 = me[2] * local_z
    bx_near = {
        1: lax.div(lax.max(start_x - 1, 0), BOX_XY),
        -1: lax.min(lax.div(start_x + own_x, BOX_XY), box_x - 1),
        0: bx0,
    }
    by_near = {
        1: lax.div(lax.rem(start_y + total_y - 1, total_y), BOX_XY),
        -1: lax.div(lax.rem(start_y + own_y, total_y), BOX_XY),
        0: by0,
    }
    bz_all = [lax.rem(bz0 + box_z + i, box_z) for i in range(-1, local_z + 1)]
    lane3 = iota((1, 1, LANES), 2)
    plane3 = iota((own_x, 1, LANES), 0)
    memo = {}

    def along_lanes(get, key, bx_key, by_key, cz):
        full = (key, bx_key, by_key, cz)
        if full in memo:
            return memo[full]
        bx, by = bx_near[bx_key], by_near[by_key]
        at = lane3 - cz
        value = jnp.full((1, 1, LANES), get(bx, by, bz_all[1]))
        for i in range(1, local_z):
            value = jnp.where(at >= i * BOX_Z, get(bx, by, bz_all[1 + i]), value)
        if cz == 1:
            value = jnp.where(at < 0, get(bx, by, bz_all[0]), value)
        elif cz == -1:
            value = jnp.where(at >= own_z, get(bx, by, bz_all[-1]), value)
        value = value.astype(jnp.float32)
        memo[full] = value
        return value

    def box_field(get, key, c):
        cx, cy, cz = c

        def on_rows(bx_key):
            own = along_lanes(get, key, bx_key, 0, cz)
            if cy == 0 or box_y == 1:
                return own
            edge = 0 if cy == 1 else own_y - 1
            return jnp.where(row3 == edge, along_lanes(get, key, bx_key, cy, cz), own)

        if cx == 0 or box_x == 1:
            return on_rows(0)
        edge = 0 if cx == 1 else own_x - 1
        return jnp.where(plane3 == edge, on_rows(cx), on_rows(0))

    def center_getter(moment, dim):
        return lambda bx, by, bz: centers[moment, dim, bx, by, bz]

    def speed_getter(dim):
        return lambda bx, by, bz: speeds[dim, bx, by, bz]

    def speeds_at(c):
        return [box_field(speed_getter(dim), ("u", dim), c) for dim in range(3)]

    def inside_at(cx):
        at = start_x + plane3 - cx
        return (at >= 0) & (at < total_x)

    def solids_at(c):
        cx, cy, cz = c
        off_x = ((start_x + plane3 - cx) & (BOX_XY - 1)).astype(jnp.float32)
        off_y = ((start_y + iota((1, SUB, LANES), 1) - cy) & (BOX_XY - 1)).astype(jnp.float32)
        off_z = ((lane3 - cz) & (BOX_Z - 1)).astype(jnp.float32)
        found = []
        for moment in range(3):
            gap_x = off_x - box_field(center_getter(moment, 0), (moment, 0), c)
            gap_y = off_y - box_field(center_getter(moment, 1), (moment, 1), c)
            gap_z = off_z - box_field(center_getter(moment, 2), (moment, 2), c)
            distance = (gap_x * gap_x + gap_z * gap_z) + gap_y * gap_y
            if cx:
                distance = jnp.where(inside_at(cx), distance, 1e9)
            found.append(jnp.where(distance <= float(RADIUS * RADIUS), 1.0, 0.0))
        return found

    own_solids = solids_at((0, 0, 0))
    for moment in range(3):
        own_masks[moment] = own_solids[moment]
    sums = [jnp.full((own_x, SUB, LANES), WEIGHTS[0], jnp.float32) for s in range(2)]
    for q in range(1, 19):
        s0, s1, s2 = solids_at(VELOCITIES[q])
        for s, (before, after) in enumerate(((s0, s1), (s1, s2))):
            free = (1.0 - before) * (1.0 - after)
            opens[s, q - 1] = free
            news[s, q - 1] = after
            sums[s] = sums[s] + WEIGHTS[q] * free
    for s in range(2):
        dens[s] = sums[s]
    own_speed = speeds_at((0, 0, 0))
    quiet = 1.0 - 1.5 * (
        own_speed[0] * own_speed[0] + own_speed[1] * own_speed[1] + own_speed[2] * own_speed[2]
    )

    def substep(s, halo, ref, density, write):
        covered = own_masks[s + 1] > 0.5
        uncovered = own_masks[s] > 0.5
        push = [jnp.zeros((own_x, SUB, LANES), jnp.float32) for d in range(3)]
        numerator = WEIGHTS[0] * density
        for q in range(1, 19):
            c = VELOCITIES[q]
            near = halo.pull(density, c, RHO + 100, own_y, own_z, 0)
            free = opens[s, q - 1]
            freed = near * free
            numerator = numerator + WEIGHTS[q] * freed
            arrived = halo.pull(ref[q], c, q, own_y, own_z, 0)
            here = (6.0 * WEIGHTS[q]) * project(own_speed, q)
            link = (2.0 * arrived - here * near) * free
            if c[0]:
                link = jnp.where(inside_at(c[0]), link, 0.0)
            for d in range(3):
                if c[d] == 1:
                    push[d] = push[d] + link
                elif c[d] == -1:
                    push[d] = push[d] - link
            wall = (6.0 * WEIGHTS[q]) * project(speeds_at(c), q)
            bounced = ref[OPPOSITE[q]] + density * wall
            arrived = jnp.where(news[s, q - 1] > 0.5, bounced, arrived)
            write(q, jnp.where(covered, ref[q], arrived))
        write(0, ref[0])
        refill = numerator / dens[s]
        replaced = uncovered & jnp.logical_not(covered)
        return refill, replaced, [jnp.where(covered, p, 0.0) for p in push]

    def refilled(refill, q):
        if q == 0:
            return refill * (WEIGHTS[0] * quiet)
        along = project(own_speed, q)
        return refill * (WEIGHTS[q] * (quiet + 3.0 * along + 4.5 * along * along))

    for copy in sends1:
        copy.wait_recv()

    def write_b(q, value):
        fine_b[q] = value

    refill, replaced, push1 = substep(0, halo1, fine_a, rho, write_b)
    for copy in sends1:
        copy.wait_send()

    def middle(q):
        return jnp.where(replaced, refilled(refill, q), fine_b[q])

    rho2 = collide(middle, write_a, FINE_RATE)
    halo2.pack(
        lambda q: rho2 if q == RHO + 100 else fine_a[q],
        fine_edges(fine_a, rho2),
        True,
        own_y,
        own_z,
        0,
    )
    sends2 = copies(halo2, 1)
    for copy in reversed(sends2):
        copy.start()

    for copy in sends_c:
        copy.wait_recv()
    for q in range(19):
        value = coarse[q]
        if q:
            value = halo1.pull(value, VELOCITIES[q], q, rows_c, lanes_c, 1)
        coarse_out[q] = value[:, 0:rows_c, 0:lanes_c]
    stores = [pltpu.make_async_copy(coarse_out, coarse_res, local_sem.at[4])]
    stores[0].start()

    for copy in sends2:
        copy.wait_recv()

    def write_b2(q, value):
        fine_b[q] = value

    refill2, replaced2, push2 = substep(1, halo2, fine_a, rho2, write_b2)

    shape = force_own.shape[1:]
    flat_at = iota(shape, 0) * LANES + iota(shape, 1)
    share = jnp.zeros(shape, jnp.float32)
    lane2 = iota((1, LANES), 1)
    for s, push in enumerate((push1, push2)):
        for d in range(3):
            column = jnp.sum(jnp.sum(push[d], axis=0), axis=0, keepdims=True)
            line = ((s * 3 + d) * box_x + bx0) * box_y + by0
            for i in range(local_z):
                within = (lane2 >= i * BOX_Z) & (lane2 < (i + 1) * BOX_Z)
                total = jnp.sum(jnp.where(within, column, 0.0), axis=1, keepdims=True)
                share = share + jnp.where(flat_at == line * box_z + bz0 + i, total, 0.0)

    reduced = []
    for number, phase in enumerate(phases):
        buffer, out_sem, in_sem = force_parts[3 * number : 3 * number + 3]
        steps = group_steps(phase, counts)
        rank = group_rank(phase, counts, me)
        force_own[number] = share
        for i, c in enumerate(steps):
            copy = pltpu.make_async_remote_copy(
                src_ref=force_own.at[number],
                dst_ref=buffer.at[rank],
                send_sem=out_sem.at[i],
                recv_sem=in_sem.at[rank],
                device_id=neighbour(c, counts, me),
                device_id_type=MESH,
            )
            copy.start()
            reduced.append(copy)
        if number == 0:
            for q in range(19):
                fine_b[q] = jnp.where(replaced2, refilled(refill2, q), fine_b[q])
            stores.append(pltpu.make_async_copy(fine_b, fine_res, local_sem.at[5]))
            stores[1].start()
        buffer[rank] = share
        for i, c in enumerate(steps):
            source = neighbour(c, counts, me)
            at = group_rank(phase, counts, source)
            pltpu.make_async_remote_copy(
                src_ref=force_own.at[number],
                dst_ref=buffer.at[at],
                send_sem=out_sem.at[i],
                recv_sem=in_sem.at[at],
                device_id=source,
                device_id_type=MESH,
            ).wait_recv()
        share = jnp.sum(buffer[...], axis=0)
    for s in range(2):
        for d in range(3):
            for bx in range(box_x):
                for by in range(box_y):
                    first_at = (((s * 3 + d) * box_x + bx) * box_y + by) * box_z
                    moved = pltpu.roll(share, -first_at % LANES, 1)
                    line = first_at // LANES
                    force_out[s, d, bx, by : by + 1, :] = moved[line : line + 1, 0:box_z]
    stores.append(pltpu.make_async_copy(force_out, force_res, local_sem.at[6]))
    stores[2].start()
    for copy in sends_c + sends2 + reduced:
        copy.wait_send()
    for copy in stores:
        copy.wait()


def force_phases(counts):
    if counts[0] * counts[1] * counts[2] <= 64:
        return ((0, 1, 2),)
    return ((0,), (1,), (2,))


def group_steps(phase, counts):
    spans = [range(counts[a]) if a in phase else range(1) for a in range(3)]
    steps = [(x, y, z) for x in spans[0] for y in spans[1] for z in spans[2]]
    return steps[1:]


def group_rank(phase, counts, at):
    rank = 0
    for a in phase:
        rank = rank * counts[a] + at[a]
    return rank


def finish(*refs):
    n = len(refs) // 2
    sem = refs[2 * n]
    outs = [pltpu.make_async_copy(refs[i], refs[n + i], sem.at[i]) for i in range(n)]
    for copy in outs:
        copy.start()
    for copy in outs:
        copy.wait()


def shards(counts, coarse_pdfs, fine_pdfs, centers, sphere_velocity):
    own_x, own_y, own_z = fine_pdfs.shape[1:]
    assert (own_x, own_y, own_z) == (4, SUB, LANES)
    assert own_z % BOX_Z == 0 and BOX_XY % own_y == 0 and BOX_XY % own_x == 0
    boxes = centers.shape[2:]
    f32 = jnp.float32
    lines = -(-6 * boxes[0] * boxes[1] * boxes[2] // LANES)
    lines = lines if lines == 1 else -(-lines // SUB) * SUB
    assert LANES % boxes[2] == 0
    phases = force_phases(counts)
    force_scratch = []
    for phase in phases:
        size = len(group_steps(phase, counts)) + 1
        force_scratch += [
            pltpu.VMEM((size, lines, LANES), f32),
            pltpu.SemaphoreType.DMA((size - 1,)),
            pltpu.SemaphoreType.DMA((size,)),
        ]

    def halo_scratch(x, y, z):
        return [
            pltpu.VMEM((2, x, SUB, LANES), f32),
            pltpu.VMEM((2, y, 1, LANES), f32),
            pltpu.VMEM((2, z, SUB, LANES), f32),
            pltpu.VMEM((2, x, SUB, LANES), f32),
            pltpu.VMEM((2, y, 1, LANES), f32),
            pltpu.VMEM((2, z, SUB, LANES), f32),
            pltpu.VMEM((4, FIRST_ROW, 1, LANES), f32),
            pltpu.VMEM((4, z, SUB, LANES), f32),
            pltpu.VMEM((4, z, SUB, LANES), f32),
        ]

    anywhere = pl.BlockSpec(memory_space=pl.ANY)
    out_shape = (
        jax.ShapeDtypeStruct(coarse_pdfs.shape, f32),
        jax.ShapeDtypeStruct(fine_pdfs.shape, f32),
        jax.ShapeDtypeStruct((2, 3) + boxes, f32),
    )
    results = pl.pallas_call(
        functools.partial(kernel, counts),
        out_shape=out_shape,
        in_specs=[pl.BlockSpec(memory_space=pltpu.HBM)] * 4,
        out_specs=(anywhere,) * 3,
        scratch_shapes=[
            pltpu.VMEM(coarse_pdfs.shape, f32),
            pltpu.VMEM(fine_pdfs.shape, f32),
            pltpu.SMEM(centers.shape, jnp.int32),
            pltpu.SMEM(sphere_velocity.shape, f32),
            pltpu.VMEM(coarse_pdfs.shape, f32),
            pltpu.VMEM((2, 3) + boxes, f32),
            pltpu.SemaphoreType.DMA((7,)),
            pltpu.VMEM((19, own_x, SUB, LANES), f32),
            pltpu.VMEM((19, own_x, SUB, LANES), f32),
            pltpu.VMEM((19, own_x, SUB, LANES), f32),
        ]
        + halo_scratch(11, ROWS, 2)
        + halo_scratch(6, COARSE_ROW, 1)
        + [
            pltpu.VMEM((2, 18, own_x, SUB, LANES), f32),
            pltpu.VMEM((2, 18, own_x, SUB, LANES), f32),
            pltpu.VMEM((3, own_x, SUB, LANES), f32),
            pltpu.VMEM((2, own_x, SUB, LANES), f32),
            pltpu.VMEM((12, SUB, LANES), f32),
            pltpu.VMEM((len(phases), lines, LANES), f32),
            pltpu.SemaphoreType.DMA((3, 18)),
            pltpu.SemaphoreType.DMA((3, 18)),
        ]
        + force_scratch,
        compiler_params=pltpu.CompilerParams(
            collective_id=0, has_side_effects=True, vmem_limit_bytes=VMEM_GRANT
        ),
    )(
        *[
            pltpu.with_memory_space_constraint(x, pltpu.HBM)
            for x in (coarse_pdfs, fine_pdfs, centers, sphere_velocity)
        ]
    )
    return pl.pallas_call(
        finish,
        out_shape=out_shape,
        in_specs=[anywhere] * 3,
        out_specs=(anywhere,) * 3,
        scratch_shapes=[pltpu.SemaphoreType.DMA((3,))],
        compiler_params=pltpu.CompilerParams(vmem_limit_bytes=VMEM_GRANT),
    )(*results)


def solution(mesh):
    counts = tuple(mesh.shape[a] for a in AXES)
    spec = P(None, "gx", "gy", "gz")
    return jax.shard_map(
        functools.partial(shards, counts),
        mesh=mesh,
        in_specs=(spec, spec, P(), P()),
        out_specs=(spec, spec, P()),
        check_vma=False,
    )
```
